768 devices in a mesh: ctx: 32 (over y, z_hi), ulysses: 24 (over x, z_lo, core).
Axes of the slice: x: 4, y: 8, z: 12 (z_hi: 4, z_lo: 3; z = z_hi * 3 + z_lo), core: 2. Of those that a mesh axis runs over, the one named last changes fastest.
Arguments:
- queries: bfloat16 [98304, 6144], P(('ctx', 'ulysses')), may hold values from -120 to 120
- keys: bfloat16 [98304, 1024], P(('ctx', 'ulysses')), may hold values from -4 to 4
- values: bfloat16 [98304, 1024], P(('ctx', 'ulysses')), may hold values from -6 to 6
- doc_ids: int32 [98304], replicated, may hold values from 0 to 191, never falling along the last dimension, each value on 1 to 768 neighbouring positions
Outputs:
- attended: bfloat16 [98304, 6144], P(('ctx', 'ulysses'))
The draws below stay inside these ranges and needn't reach their ends.
Inputs may be any that keep to these rules, and one draw needn't show every extreme that they name: `doc_ids`: document numbers never fall along the tokens; every document holds at most 768 tokens and one holds exactly that many.
All inputs are finite; a program needn't handle non-finite values.
Results may differ from the reference program's by a relative error of at most 0.001.
Values may be sent and summed in bfloat16 or wider, within the bound.
A program may use at most 64 MiB of HBM per device.

```python
import math
import jax
import jax.numpy as jnp
import numpy as np
from jax import lax

HQ = 48
KV = 8
HEAD = 128
BLOCK = 3072
TOKENS = 98304
DOCS = 192
MOST_DOC = 768


def draw_pair(key):
    key_set = jnp.clip(jax.random.normal(jax.random.fold_in(key, 11), (TOKENS, KV, HEAD), jnp.float32), -4.0, 4.0)
    query_set = jnp.clip(jax.random.normal(jax.random.fold_in(key, 12), (TOKENS, HQ, HEAD), jnp.float32), -4.0, 4.0)
    return (query_set, key_set)


def draw_queries(key, part):
    query_set, key_set = draw_pair(key)
    return query_set.reshape(TOKENS, HQ * HEAD).astype(jnp.bfloat16)


def draw_keys(key, part):
    query_set, key_set = draw_pair(key)
    return key_set.reshape(TOKENS, KV * HEAD).astype(jnp.bfloat16)


def block_levels(key, dims, cuts, least, top_value):
    def one(position, parts):
        draws = jax.random.uniform(jax.random.fold_in(jax.random.fold_in(key, 6), position), (parts,), jnp.float32, least / len(cuts), top_value / len(cuts))
        return jnp.repeat(jnp.exp(draws), dims[position] // parts).reshape((-1,) + (1,) * (len(dims) - position - 1))

    gain = one(*cuts[0])
    for cut in cuts[1:]:
        gain = gain * one(*cut)
    return gain


def split_up(amount, total, most, slope):
    weights = [(1 << 20) // math.isqrt(rank ** slope) + 1 for rank in range(2, amount + 1)]
    spare, holding = total - most - (amount - 1), [1] * (amount - 1)
    while spare > 0:
        free = [i for i in range(amount - 1) if holding[i] < most]
        pool, left = sum([weights[i] for i in free]), spare
        for i in free:
            extra = min(most - holding[i], max(1, left * weights[i] // pool), spare)
            holding[i] = holding[i] + extra
            spare = spare - extra
    return np.array([most] + holding)


def uneven(own_key, number_of, total, bound, lean):
    if number_of == 2:
        one = jax.random.randint(own_key, (), max(1, total - bound), min(bound, total - 1) + 1)
        return jnp.stack([one, total - one])
    tallies = jnp.asarray(split_up(number_of, total, bound, lean), jnp.int32)
    twos = (number_of - 1) // 2
    source_of, taker = tallies[1:1 + 2 * twos:2], tallies[2:2 + 2 * twos:2]
    slack = jnp.minimum(source_of - 1, bound - taker)
    moved = jax.random.randint(jax.random.fold_in(own_key, 1), (twos,), 0, 1 << 20) % (slack + 1)
    tallies = tallies.at[1:1 + 2 * twos:2].set(source_of - moved).at[2:2 + 2 * twos:2].set(taker + moved)
    return tallies[jax.random.permutation(jax.random.fold_in(own_key, 2), number_of)]


def centred(stream_key, extent, spread, limit, shards=(), held_as=jnp.bfloat16):
    loudness = block_levels(stream_key, extent, shards, -0.22, 0.18) if shards else 1.0
    result = jax.random.normal(stream_key, extent, jnp.float32) * spread * loudness
    return jnp.minimum(jnp.maximum(result, -limit), limit).astype(held_as)


def setup_inputs(seed: int = 0) -> dict:
    key_list = jax.random.split(jax.random.key(seed), 5)
    queries = draw_queries(jax.random.fold_in(key_list[4], 71), 0)
    keys = draw_keys(jax.random.fold_in(key_list[4], 71), 0)
    values = centred(key_list[2], (TOKENS, KV * HEAD), 1.0, 6.0, ((0, 768),))
    doc_ids = jnp.searchsorted(jnp.cumsum(uneven(key_list[3], DOCS, TOKENS, MOST_DOC, 1)), jnp.arange(TOKENS), side="right").astype(jnp.int32)
    return dict(queries=queries, keys=keys, values=values, doc_ids=doc_ids)


def reference(queries, keys, values, doc_ids):
    scale_factor = 1.0 / math.sqrt(HEAD)
    group_size = HQ // KV
    reach = MOST_DOC
    sub_rows = 512 if TOKENS % 512 == 0 else BLOCK
    window = reach + sub_rows
    key_pad = jnp.concatenate([jnp.zeros((reach, KV * HEAD), keys.dtype), keys], axis=0)
    value_pad = jnp.concatenate([jnp.zeros((reach, KV * HEAD), values.dtype), values], axis=0)
    doc_pad = jnp.concatenate([jnp.full((reach,), -1, jnp.int32), doc_ids.astype(jnp.int32)], axis=0)

    def one_block(number):
        first_row = (number * sub_rows).astype(jnp.int32)
        query_part = lax.dynamic_slice_in_dim(queries, first_row, sub_rows, 0).reshape(sub_rows, KV, group_size, HEAD)
        key_part = lax.dynamic_slice_in_dim(key_pad, first_row, window, 0).reshape(window, KV, HEAD)
        value_part = lax.dynamic_slice_in_dim(value_pad, first_row, window, 0).reshape(window, KV, HEAD)
        query_doc = lax.dynamic_slice_in_dim(doc_ids.astype(jnp.int32), first_row, sub_rows, 0)
        key_doc = lax.dynamic_slice_in_dim(doc_pad, first_row, window, 0)
        query_pos = first_row + jnp.arange(sub_rows, dtype=jnp.int32)
        key_pos = first_row - reach + jnp.arange(window, dtype=jnp.int32)
        visible = (key_doc[None, :] == query_doc[:, None]) & (key_pos[None, :] <= query_pos[:, None])

        def one_head(operands):
            query_head, key_head, value_head = operands
            scores = jnp.einsum('bgd,wd->gbw', query_head.astype(jnp.float32), key_head.astype(jnp.float32)) * scale_factor
            scores = jnp.where(visible[None], scores, -jnp.inf)
            peak = lax.optimization_barrier(jnp.max(scores, axis=-1, keepdims=True))
            weights = jnp.exp(scores - peak)
            totals = lax.optimization_barrier(jnp.sum(weights, axis=-1))
            rounded = lax.optimization_barrier(weights.astype(jnp.bfloat16)).astype(jnp.float32)
            mixed = jnp.einsum('gbw,wd->bgd', rounded, value_head.astype(jnp.float32))
            return mixed / jnp.transpose(totals, (1, 0))[..., None]
        mixed = lax.map(one_head, (jnp.transpose(query_part, (1, 0, 2, 3)), jnp.transpose(key_part, (1, 0, 2)), jnp.transpose(value_part, (1, 0, 2))))
        return jnp.transpose(mixed, (1, 0, 2, 3)).reshape(sub_rows, HQ * HEAD).astype(jnp.bfloat16)
    blocks = lax.map(one_block, jnp.arange(TOKENS // sub_rows, dtype=jnp.int32))
    return blocks.reshape(TOKENS, HQ * HEAD)
```

```python
import math

import jax
import jax.numpy as jnp
from jax import lax
from jax.experimental import pallas as pl
from jax.experimental.pallas import tpu as pltpu
from jax.sharding import PartitionSpec as P

HQ = 48
KV = 8
HEAD = 128
PER = HQ // KV
CHUNK = 128
BACK = 6
SLOTS = BACK + 1
WINDOW = SLOTS * CHUNK
SCALE2 = math.log2(math.e) / math.sqrt(HEAD)
MESH = pl.DeviceIdType.MESH


def kernel(
    n_ctx, n_chip, q_hbm, k_hbm, v_hbm, doc_hbm, o_hbm,
    kv, qbuf, obuf, docs, bias, s_ref, p_ref,
    load_sem, q_sem, doc_sem, ici_send, pair_send, recv_sem, out_sem,
):
    ctx = lax.axis_index("ctx")
    uly = lax.axis_index("ulysses")
    lane = lax.rem(uly, 2)
    chip = ctx * n_chip + uly // 2
    chips = n_ctx * n_chip
    chunk = chip * 2 + lane
    ahead = lax.rem(chip + 1, chips)
    behind = lax.rem(chip + chips - 1, chips)
    next_id = (ahead // n_chip, lax.rem(ahead, n_chip) * 2 + lane)
    prev_id = (behind // n_chip, lax.rem(behind, n_chip) * 2 + lane)
    pair_id = (ctx, uly + 1 - 2 * lane)

    def own_load(h, part):
        src = (k_hbm, v_hbm)[part]
        return pltpu.make_async_copy(
            src.at[:, pl.ds(h * HEAD, HEAD)],
            kv.at[h, part, pl.ds(BACK * CHUNK, CHUNK), :],
            load_sem.at[part, h],
        )

    for h in range(KV):
        own_load(h, 0).start()
        own_load(h, 1).start()
    doc_load = pltpu.make_async_copy(doc_hbm, docs, doc_sem)
    doc_load.start()
    q_load = pltpu.make_async_copy(q_hbm, qbuf, q_sem)
    q_load.start()

    barrier = pltpu.get_barrier_semaphore()
    for who in (prev_id, pair_id):
        pl.semaphore_signal(barrier, inc=1, device_id=who, device_id_type=MESH)
    pl.semaphore_wait(barrier, 2)

    def rows(slot):
        return pl.ds(pl.multiple_of(slot * CHUNK, CHUNK), CHUNK)

    def hop(h, stage):
        src, dst = BACK - 2 * stage, BACK - 2 * stage - 2
        return pltpu.make_async_remote_copy(
            src_ref=kv.at[h, :, rows(src), :],
            dst_ref=kv.at[h, :, rows(dst), :],
            send_sem=ici_send.at[stage, h],
            recv_sem=recv_sem.at[dst, h],
            device_id=next_id,
            device_id_type=MESH,
        )

    def across(h, stage):
        src, dst = BACK - 2 * stage - 2 * lane, BACK - 2 * stage - 1
        return pltpu.make_async_remote_copy(
            src_ref=kv.at[h, :, rows(src), :],
            dst_ref=kv.at[h, :, rows(dst), :],
            send_sem=pair_send.at[stage, h],
            recv_sem=recv_sem.at[dst, h],
            device_id=pair_id,
            device_id_type=MESH,
        )

    def send_own(h):
        own_load(h, 0).wait()
        own_load(h, 1).wait()
        hop(h, 0).start()

    for h in range(2):
        send_own(h)

    doc_load.wait()
    own_doc = docs[pl.ds(chunk, 1), :]
    query_doc = jnp.transpose(jnp.broadcast_to(own_doc, (CHUNK, CHUNK)))
    row = lax.broadcasted_iota(jnp.int32, (CHUNK, CHUNK), 0)
    col = lax.broadcasted_iota(jnp.int32, (CHUNK, CHUNK), 1)
    for slot in range(SLOTS):
        where = chunk - (BACK - slot)
        key_doc = docs[pl.ds(jnp.maximum(where, 0), 1), :]
        visible = query_doc == jnp.broadcast_to(key_doc, (CHUNK, CHUNK))
        if slot == BACK:
            visible = visible & (col <= row)
        else:
            visible = visible & (jnp.broadcast_to(where, (CHUNK, CHUNK)) >= 0)
        bias[:, slot * CHUNK : (slot + 1) * CHUNK] = jnp.where(visible, 0.0, -1e30).astype(jnp.float32)
    q_load.wait()

    def out_copy(h):
        cols = pl.ds(pl.multiple_of(h * (PER * HEAD), PER * HEAD), PER * HEAD)
        return pltpu.make_async_copy(obuf.at[:, cols], o_hbm.at[:, cols], out_sem.at[h])

    def attend(h):
        base = h * (PER * HEAD)
        q_all = jnp.concatenate(
            [qbuf[:, pl.ds(pl.multiple_of(base + r * HEAD, HEAD), HEAD)] for r in range(PER)], axis=0
        )
        for first in range(0, WINDOW, 256):
            width = min(256, WINDOW - first)
            block = lax.dot_general(
                q_all, kv[h, 0, first : first + width, :], (((1,), (1,)), ((), ())),
                preferred_element_type=jnp.float32,
            )
            for r in range(PER):
                s_ref[r * CHUNK : (r + 1) * CHUNK, first : first + width] = (
                    block[r * CHUNK : (r + 1) * CHUNK] + bias[:, first : first + width]
                )
        totals = []
        step = 32
        for r in range(0, PER * CHUNK, step):
            scores = s_ref[r : r + step, :]
            peak = jnp.max(scores, axis=-1, keepdims=True)
            weights = jnp.exp2((scores - peak) * SCALE2)
            totals.append(jnp.sum(weights, axis=-1, keepdims=True))
            p_ref[r : r + step, :] = weights.astype(jnp.bfloat16)
        mixed = jnp.dot(p_ref[...], kv[h, 1], preferred_element_type=jnp.float32)
        done = (mixed / jnp.concatenate(totals, axis=0)).astype(jnp.bfloat16)
        for r in range(PER):
            obuf[:, pl.ds(pl.multiple_of(base + r * HEAD, HEAD), HEAD)] = done[r * CHUNK : (r + 1) * CHUNK]
        out_copy(h).start()

    def step(t, carry):
        @pl.when(t + 2 < KV)
        def _():
            send_own(t + 2)

        @pl.when(t < KV)
        def _():
            hop(t, 0).wait_recv()
            hop(t, 1).start()
            across(t, 0).start()

        @pl.when((t >= 1) & (t < KV + 1))
        def _():
            h = t - 1
            hop(h, 1).wait_recv()
            hop(h, 2).start()
            across(h, 1).start()

        @pl.when((t >= 2) & (t < KV + 2))
        def _():
            h = t - 2
            hop(h, 2).wait_recv()
            across(h, 2).start()

        @pl.when(t >= 3)
        def _():
            h = t - 3
            for stage in range(3):
                across(h, stage).wait_recv()
            attend(h)

        return carry

    lax.fori_loop(0, KV + 3, step, 0)

    def drain(h, carry):
        for stage in range(3):
            hop(h, stage).wait_send()
            across(h, stage).wait_send()
        out_copy(h).wait()
        return carry

    lax.fori_loop(0, KV, drain, 0)


def shards(n_ctx, n_chip, queries, keys, values, doc_ids):
    tokens = queries.shape[0]
    anywhere = pl.BlockSpec(memory_space=pl.ANY)
    docs = doc_ids.reshape(-1, CHUNK)
    return pl.pallas_call(
        lambda *refs: kernel(n_ctx, n_chip, *refs),
        out_shape=jax.ShapeDtypeStruct((tokens, HQ * HEAD), jnp.bfloat16),
        in_specs=[anywhere] * 4,
        out_specs=anywhere,
        scratch_shapes=[
            pltpu.VMEM((KV, 2, WINDOW, HEAD), jnp.bfloat16),
            pltpu.VMEM((CHUNK, HQ * HEAD), jnp.bfloat16),
            pltpu.VMEM((CHUNK, HQ * HEAD), jnp.bfloat16),
            pltpu.VMEM(docs.shape, jnp.int32),
            pltpu.VMEM((CHUNK, WINDOW), jnp.float32),
            pltpu.VMEM((PER * CHUNK, WINDOW), jnp.float32),
            pltpu.VMEM((PER * CHUNK, WINDOW), jnp.bfloat16),
            pltpu.SemaphoreType.DMA((2, KV)),
            pltpu.SemaphoreType.DMA,
            pltpu.SemaphoreType.DMA,
            pltpu.SemaphoreType.DMA((3, KV)),
            pltpu.SemaphoreType.DMA((3, KV)),
            pltpu.SemaphoreType.DMA((BACK, KV)),
            pltpu.SemaphoreType.DMA((KV,)),
        ],
        compiler_params=pltpu.CompilerParams(
            collective_id=0, has_side_effects=True, vmem_limit_bytes=56 * 1024 * 1024
        ),
        name="halo_attention",
    )(queries, keys, values, docs)


def solution(mesh):
    placed = (
        P(("ctx", "ulysses"), None),
        P(("ctx", "ulysses"), None),
        P(("ctx", "ulysses"), None),
        P(),
    )
    n_ctx, n_chip = mesh.shape["ctx"], mesh.shape["ulysses"] // 2
    return jax.shard_map(
        lambda *arrays: shards(n_ctx, n_chip, *arrays),
        mesh=mesh, in_specs=placed, out_specs=P(("ctx", "ulysses"), None), check_vma=False,
    )
```

```python
import math

import jax
import jax.numpy as jnp
from jax import lax
from jax.experimental import pallas as pl
from jax.experimental.pallas import tpu as pltpu
from jax.sharding import PartitionSpec as P

HQ = 48
KV = 8
HEAD = 128
PER = HQ // KV
CHUNK = 128
BACK = 6
SLOTS = BACK + 1
WINDOW = SLOTS * CHUNK
SCALE2 = math.log2(math.e) / math.sqrt(HEAD)
RUN = 3
LAGS_IN = (0, 2, 1, 3)
LAGS_TOP = (1, 3, 5, 6)
LAGS_HELD = (3, 1, 0)
MESH = pl.DeviceIdType.MESH


def kernel(
    n_ctx, n_chip, q_hbm, k_hbm, v_hbm, doc_hbm, o_hbm,
    kv, held, qbuf, obuf, docs, bias, s_ref, p_ref,
    load_sem, q_sem, doc_sem, push_send, held_send, pair_send, recv_sem, held_recv, out_sem,
):
    ctx = lax.axis_index("ctx")
    uly = lax.axis_index("ulysses")
    lane = lax.rem(uly, 2)
    place = uly // 2
    row, col = place // RUN, lax.rem(place, RUN)
    last_row = n_chip // RUN - 1
    chip = ctx * n_chip + place
    chunk = chip * 2 + lane
    top, inner = row == 0, row > 0
    edge = (row == last_row) & (col == RUN - 1)
    onward = ctx < n_ctx - 1
    edge_far = edge & onward & (lane == 0)
    edge_near = edge & onward & (lane == 1)
    keeper = top & (col == RUN - 1) & onward & (lane == 0)
    holder = chip - (n_chip - RUN)
    after = chip + (n_chip - RUN + 1)

    def core(target):
        return (target // n_chip, lax.rem(target, n_chip) * 2 + lane)

    pair_id = (ctx, uly + 1 - 2 * lane)

    def own_load(h, part):
        src = (k_hbm, v_hbm)[part]
        return pltpu.make_async_copy(
            src.at[:, pl.ds(pl.multiple_of(h * HEAD, HEAD), HEAD)],
            kv.at[h, part, pl.ds(BACK * CHUNK, CHUNK), :],
            load_sem.at[part, h],
        )

    def start_loads(h, carry):
        own_load(h, 0).start()
        own_load(h, 1).start()
        return carry

    lax.fori_loop(0, KV, start_loads, 0)
    doc_load = pltpu.make_async_copy(doc_hbm, docs, doc_sem)
    doc_load.start()
    q_load = pltpu.make_async_copy(q_hbm, qbuf, q_sem)
    q_load.start()

    @pl.when(chip < 3)
    def _():
        def clear(h, carry):
            for part in range(2):
                kv[h, part, : BACK * CHUNK, :] = jnp.zeros((BACK * CHUNK, HEAD), jnp.bfloat16)
            return carry

        lax.fori_loop(0, KV, clear, 0)

    def rows(slot):
        return pl.ds(pl.multiple_of(slot * CHUNK, CHUNK), CHUNK)

    def push(h, src, dst, index, target):
        return pltpu.make_async_remote_copy(
            src_ref=kv.at[h, :, rows(src), :],
            dst_ref=kv.at[h, :, rows(dst), :],
            send_sem=push_send.at[index, h],
            recv_sem=recv_sem.at[dst, h],
            device_id=core(target),
            device_id_type=MESH,
        )

    def push_held(h, src, index):
        return pltpu.make_async_remote_copy(
            src_ref=kv.at[h, :, rows(src), :],
            dst_ref=held.at[h, src // 2 - 1],
            send_sem=push_send.at[index, h],
            recv_sem=held_recv.at[src // 2 - 1, h],
            device_id=core(holder),
            device_id_type=MESH,
        )

    def release(h, index):
        dst = 2 * index
        return pltpu.make_async_remote_copy(
            src_ref=held.at[h, index],
            dst_ref=kv.at[h, :, rows(dst), :],
            send_sem=held_send.at[index, h],
            recv_sem=recv_sem.at[dst, h],
            device_id=core(after),
            device_id_type=MESH,
        )

    def across(h, stage):
        src, dst = BACK - 2 * stage - 2 * lane, BACK - 2 * stage - 1
        return pltpu.make_async_remote_copy(
            src_ref=kv.at[h, :, rows(src), :],
            dst_ref=kv.at[h, :, rows(dst), :],
            send_sem=pair_send.at[stage, h],
            recv_sem=recv_sem.at[dst, h],
            device_id=pair_id,
            device_id_type=MESH,
        )

    own_next = jnp.logical_not(edge) | edge_near
    own_row = row < last_row
    own_skip = (col == RUN - 1) & (own_row | edge_near)
    relay_up = (col == 1) | (top & (col == 0) & (lane == 0)) | edge_near
    relay_two = edge_near
    relay_three = (top & (col == 1)) | (top & (col == 0) & (lane == 0)) | edge_near
    relay_down = inner & (col == 1)

    barrier = pltpu.get_barrier_semaphore()

    def greet(cond, target):
        @pl.when(cond)
        def _():
            pl.semaphore_signal(barrier, inc=1, device_id=core(target), device_id_type=MESH)

    head_of_block = top & (col == 0)
    has_back = ctx > 0
    greet((chip >= 1) & jnp.logical_not(head_of_block & (lane == 0)), chip - 1)
    greet(inner, chip - RUN)
    greet((inner & (col == 1)) | (top & (col == 1) & has_back & (lane == 1)), chip - 2)
    greet(inner & (col == 0), chip + 1)
    greet(keeper, chip + (n_chip - RUN))
    greet(head_of_block & has_back & (lane == 0), chip - (n_chip - RUN + 1))
    pl.semaphore_signal(barrier, inc=1, device_id=pair_id, device_id_type=MESH)
    expected = (
        1
        + own_next.astype(jnp.int32)
        + own_row.astype(jnp.int32)
        + own_skip.astype(jnp.int32)
        + relay_down.astype(jnp.int32)
        + edge_far.astype(jnp.int32)
        + keeper.astype(jnp.int32)
    )
    pl.semaphore_wait(barrier, expected)

    def send_own(h):
        own_load(h, 0).wait()
        own_load(h, 1).wait()

        @pl.when(own_next)
        def _():
            push(h, 6, 4, 0, chip + 1).start()

        @pl.when(edge_far)
        def _():
            push_held(h, 6, 0).start()

        @pl.when(own_skip)
        def _():
            push(h, 6, 2, 2, chip + 2).start()

        @pl.when(own_row)
        def _():
            push(h, 6, 0, 1, chip + 3).start()

        @pl.when(lane == 0)
        def _():
            across(h, 0).start()

    def received(h, slot):
        push(h, 6, slot, 0, chip).wait_recv()

    upfront = jnp.where((col == 1) & inner, 2, KV)

    def first_sends(h, carry):
        send_own(h)
        return carry

    lax.fori_loop(0, upfront, first_sends, 0)

    doc_load.wait()
    own_doc = docs[pl.ds(chunk, 1), :]
    query_doc = jnp.transpose(jnp.broadcast_to(own_doc, (CHUNK, CHUNK)))
    i = lax.broadcasted_iota(jnp.int32, (CHUNK, CHUNK), 0)
    j = lax.broadcasted_iota(jnp.int32, (CHUNK, CHUNK), 1)
    for slot in range(SLOTS):
        where = chunk - (BACK - slot)
        key_doc = docs[pl.ds(jnp.maximum(where, 0), 1), :]
        visible = query_doc == jnp.broadcast_to(key_doc, (CHUNK, CHUNK))
        if slot == BACK:
            visible = visible & (j <= i)
        else:
            visible = visible & (jnp.broadcast_to(where, (CHUNK, CHUNK)) >= 0)
        bias[:, slot * CHUNK : (slot + 1) * CHUNK] = jnp.where(visible, 0.0, -1e30).astype(jnp.float32)
    q_load.wait()

    def out_copy(h):
        cols = pl.ds(pl.multiple_of(h * (PER * HEAD), PER * HEAD), PER * HEAD)
        return pltpu.make_async_copy(obuf.at[:, cols], o_hbm.at[:, cols], out_sem.at[h])

    def attend(h):
        base = h * (PER * HEAD)
        q_all = jnp.concatenate(
            [qbuf[:, pl.ds(pl.multiple_of(base + r * HEAD, HEAD), HEAD)] for r in range(PER)], axis=0
        )
        for first in range(0, WINDOW, 256):
            width = min(256, WINDOW - first)
            block = lax.dot_general(
                q_all, kv[h, 0, first : first + width, :], (((1,), (1,)), ((), ())),
                preferred_element_type=jnp.float32,
            )
            for r in range(PER):
                s_ref[r * CHUNK : (r + 1) * CHUNK, first : first + width] = (
                    block[r * CHUNK : (r + 1) * CHUNK] + bias[:, first : first + width]
                )
        totals = []
        step = 32
        for r in range(0, PER * CHUNK, step):
            scores = s_ref[r : r + step, :]
            peak = jnp.max(scores, axis=-1, keepdims=True)
            weights = jnp.exp2((scores - peak) * SCALE2)
            totals.append(jnp.sum(weights, axis=-1, keepdims=True))
            p_ref[r : r + step, :] = weights.astype(jnp.bfloat16)
        mixed = jnp.dot(p_ref[...], kv[h, 1], preferred_element_type=jnp.float32)
        done = (mixed / jnp.concatenate(totals, axis=0)).astype(jnp.bfloat16)
        for r in range(PER):
            obuf[:, pl.ds(pl.multiple_of(base + r * HEAD, HEAD), HEAD)] = done[r * CHUNK : (r + 1) * CHUNK]
        out_copy(h).start()

    def on_near(h):
        @pl.when(chip >= 1)
        def _():
            received(h, 4)

            @pl.when(relay_up)
            def _():
                push(h, 4, 2, 3, chip + 1).start()

            @pl.when(edge_far)
            def _():
                push_held(h, 4, 3).start()

            @pl.when(relay_two)
            def _():
                push(h, 4, 0, 4, chip + 2).start()

            across(h, 1 - lane).start()

    def on_middle(h):
        @pl.when(chip >= 2)
        def _():
            received(h, 2)

            @pl.when(relay_three)
            def _():
                push(h, 2, 0, 5, chip + 1).start()

            @pl.when(edge_far)
            def _():
                push_held(h, 2, 5).start()

            across(h, 2 - lane).start()

    def on_far(h):
        @pl.when(chip >= 3)
        def _():
            received(h, 0)

            @pl.when(relay_down)
            def _():
                push(h, 0, 2, 6, chip - 1).start()

            @pl.when(lane == 1)
            def _():
                across(h, 2).start()

    def on_held(h, index):
        push_held(h, 2 * index + 2, 0).wait_recv()
        release(h, index).start()

    def inside(h):
        return (h >= 0) & (h < KV)

    def at(t, lag, action, extra=None):
        h = t - lag
        cond = inside(h) if extra is None else inside(h) & extra

        @pl.when(cond)
        def _():
            action(h)

    lag_near = jnp.where(top, LAGS_TOP[0], LAGS_IN[0])
    lag_middle = jnp.where(top, LAGS_TOP[1], LAGS_IN[1])
    lag_far = jnp.where(top, LAGS_TOP[2], LAGS_IN[2])
    lag_attend = jnp.where(top, LAGS_TOP[3], LAGS_IN[3])

    def finish(h):
        for stage in range(3):
            @pl.when(chip >= stage + 1 - lane)
            def _():
                across(h, stage).wait_recv()
        attend(h)

    def step(t, carry):
        at(t, -upfront, send_own)
        at(t, lag_near, on_near)
        at(t, LAGS_HELD[2], lambda h: on_held(h, 2), keeper)
        at(t, LAGS_HELD[1], lambda h: on_held(h, 1), keeper)
        at(t, LAGS_HELD[0], lambda h: on_held(h, 0), keeper)
        at(t, lag_far, on_far, inner)
        at(t, lag_middle, on_middle)
        at(t, lag_far, on_far, top)
        at(t, lag_attend, finish)
        return carry

    lax.fori_loop(0, KV + lag_attend, step, 0)

    def drain(h, carry):
        sends = (
            (0, own_next | edge_far), (1, own_row), (2, own_skip),
            (3, (chip >= 1) & (relay_up | edge_far)), (4, relay_two),
            (5, (chip >= 2) & (relay_three | edge_far)), (6, relay_down),
        )
        for index, cond in sends:
            @pl.when(cond)
            def _():
                push(h, 6, 4, index, chip).wait_send()

        for index in range(3):
            @pl.when(keeper)
            def _():
                release(h, index).wait_send()

        for stage in range(3):
            @pl.when(chip >= stage + lane)
            def _():
                across(h, stage).wait_send()

        out_copy(h).wait()
        return carry

    lax.fori_loop(0, KV, drain, 0)


def shards(n_ctx, n_chip, queries, keys, values, doc_ids):
    tokens = queries.shape[0]
    anywhere = pl.BlockSpec(memory_space=pl.ANY)
    docs = doc_ids.reshape(-1, CHUNK)
    return pl.pallas_call(
        lambda *refs: kernel(n_ctx, n_chip, *refs),
        out_shape=jax.ShapeDtypeStruct((tokens, HQ * HEAD), jnp.bfloat16),
        in_specs=[anywhere] * 4,
        out_specs=anywhere,
        scratch_shapes=[
            pltpu.VMEM((KV, 2, WINDOW, HEAD), jnp.bfloat16),
            pltpu.VMEM((KV, 3, 2, CHUNK, HEAD), jnp.bfloat16),
            pltpu.VMEM((CHUNK, HQ * HEAD), jnp.bfloat16),
            pltpu.VMEM((CHUNK, HQ * HEAD), jnp.bfloat16),
            pltpu.VMEM(docs.shape, jnp.int32),
            pltpu.VMEM((CHUNK, WINDOW), jnp.float32),
            pltpu.VMEM((PER * CHUNK, WINDOW), jnp.float32),
            pltpu.VMEM((PER * CHUNK, WINDOW), jnp.bfloat16),
            pltpu.SemaphoreType.DMA((2, KV)),
            pltpu.SemaphoreType.DMA,
            pltpu.SemaphoreType.DMA,
            pltpu.SemaphoreType.DMA((7, KV)),
            pltpu.SemaphoreType.DMA((3, KV)),
            pltpu.SemaphoreType.DMA((3, KV)),
            pltpu.SemaphoreType.DMA((BACK, KV)),
            pltpu.SemaphoreType.DMA((3, KV)),
            pltpu.SemaphoreType.DMA((KV,)),
        ],
        compiler_params=pltpu.CompilerParams(
            collective_id=0, has_side_effects=True, vmem_limit_bytes=56 * 1024 * 1024
        ),
        name="halo_attention",
    )(queries, keys, values, docs)


def solution(mesh):
    placed = (
        P(("ctx", "ulysses"), None),
        P(("ctx", "ulysses"), None),
        P(("ctx", "ulysses"), None),
        P(),
    )
    n_ctx, n_chip = mesh.shape["ctx"], mesh.shape["ulysses"] // 2
    return jax.shard_map(
        lambda *arrays: shards(n_ctx, n_chip, *arrays),
        mesh=mesh, in_specs=placed, out_specs=P(("ctx", "ulysses"), None), check_vma=False,
    )
```

```python
import math

import jax
import jax.numpy as jnp
from jax import lax
from jax.experimental import pallas as pl
from jax.experimental.pallas import tpu as pltpu
from jax.sharding import PartitionSpec as P

HQ = 48
KV = 8
HEAD = 128
PER = HQ // KV
CHUNK = 128
BACK = 6
SLOTS = BACK + 1
WINDOW = SLOTS * CHUNK
SCALE2 = math.log2(math.e) / math.sqrt(HEAD)
RUN = 3
LAGS_IN = (0, 2, 1, 3)
LAGS_TOP = (1, 3, 5, 6)
AHEAD = 3
LAGS_HELD = (3, 1, 0)
LAG_LATE = 8
TURNS = 4
MESH = pl.DeviceIdType.MESH


def kernel(
    n_ctx, n_chip, q_hbm, k_hbm, v_hbm, doc_hbm, o_hbm,
    kv, held, qbuf, obuf, docs, bias, s_ref, p_ref,
    load_sem, q_sem, doc_sem, push_send, held_send, pair_send, recv_sem, held_recv, out_sem,
):
    ctx = lax.axis_index("ctx")
    uly = lax.axis_index("ulysses")
    lane = lax.rem(uly, 2)
    place = uly // 2
    row, col = place // RUN, lax.rem(place, RUN)
    last_row = n_chip // RUN - 1
    chip = ctx * n_chip + place
    chunk = chip * 2 + lane
    top, inner = row == 0, row > 0
    edge = (row == last_row) & (col == RUN - 1)
    onward = ctx < n_ctx - 1
    edge_far = edge & onward & (lane == 0)
    edge_near = edge & onward & (lane == 1)
    keeper = (row == 1) & (col == RUN - 1) & onward & (lane == 0)
    to_keeper = n_chip - 2 * RUN
    from_keeper = n_chip - 2 * RUN + 1

    def core(away):
        there = place + away
        wrap = (there >= n_chip).astype(jnp.int32) - (there < 0).astype(jnp.int32)
        return (ctx + wrap, uly + 2 * away - 2 * n_chip * wrap)

    pair_id = (ctx, uly + 1 - 2 * lane)

    def own_load(h, part):
        src = (k_hbm, v_hbm)[part]
        return pltpu.make_async_copy(
            src.at[:, pl.ds(pl.multiple_of(h * HEAD, HEAD), HEAD)],
            kv.at[h, part, pl.ds(BACK * CHUNK, CHUNK), :],
            load_sem.at[part, h],
        )

    def start_loads(h, carry):
        own_load(h, 0).start()
        own_load(h, 1).start()
        return carry

    lax.fori_loop(0, KV, start_loads, 0)
    doc_load = pltpu.make_async_copy(doc_hbm, docs, doc_sem)
    doc_load.start()
    q_load = pltpu.make_async_copy(q_hbm, qbuf, q_sem)
    q_load.start()

    @pl.when(chip < 3)
    def _():
        def clear(h, carry):
            for part in range(2):
                kv[h, part, : BACK * CHUNK, :] = jnp.zeros((BACK * CHUNK, HEAD), jnp.bfloat16)
            return carry

        lax.fori_loop(0, KV, clear, 0)

    def rows(slot):
        return pl.ds(pl.multiple_of(slot * CHUNK, CHUNK), CHUNK)

    def push(h, src, dst, index, target):
        return pltpu.make_async_remote_copy(
            src_ref=kv.at[h, :, rows(src), :],
            dst_ref=kv.at[h, :, rows(dst), :],
            send_sem=push_send.at[index, h],
            recv_sem=recv_sem.at[dst, h],
            device_id=core(target),
            device_id_type=MESH,
        )

    def push_spare(h):
        return pltpu.make_async_remote_copy(
            src_ref=kv.at[h, :, rows(6), :],
            dst_ref=held.at[h, 0],
            send_sem=push_send.at[2, h],
            recv_sem=held_recv.at[0, h],
            device_id=core(-to_spare),
            device_id_type=MESH,
        )

    def release_spare(h):
        return pltpu.make_async_remote_copy(
            src_ref=held.at[h, 0],
            dst_ref=kv.at[h, :, rows(0), :],
            send_sem=held_send.at[0, h],
            recv_sem=recv_sem.at[0, h],
            device_id=core(from_spare),
            device_id_type=MESH,
        )

    def push_held(h, src, index):
        return pltpu.make_async_remote_copy(
            src_ref=kv.at[h, :, rows(src), :],
            dst_ref=held.at[h, src // 2 - 1],
            send_sem=push_send.at[index, h],
            recv_sem=held_recv.at[src // 2 - 1, h],
            device_id=core(-to_keeper),
            device_id_type=MESH,
        )

    def release(h, index):
        dst = 2 * index
        return pltpu.make_async_remote_copy(
            src_ref=held.at[h, index],
            dst_ref=kv.at[h, :, rows(dst), :],
            send_sem=held_send.at[index, h],
            recv_sem=recv_sem.at[dst, h],
            device_id=core(from_keeper),
            device_id_type=MESH,
        )

    def across(h, stage):
        src, dst = BACK - 2 * stage - 2 * lane, BACK - 2 * stage - 1
        return pltpu.make_async_remote_copy(
            src_ref=kv.at[h, :, rows(src), :],
            dst_ref=kv.at[h, :, rows(dst), :],
            send_sem=pair_send.at[stage, h],
            recv_sem=recv_sem.at[dst, h],
            device_id=pair_id,
            device_id_type=MESH,
        )

    own_next = jnp.logical_not(edge) | edge_near
    own_row = row < last_row
    plane_out = lax.rem(ctx, TURNS) == TURNS - 1
    plane_in = lax.rem(ctx, TURNS) == 0
    direct = edge_near & jnp.logical_not(plane_out)
    chained = top & (col == 0) & (lane == 0)
    chained_two = top & (col == 0) & ((lane == 0) | plane_in)
    cross_plane = plane_out & onward
    spare_source = (row == last_row) & (col == 0) & cross_plane
    spare_keeper = (row == 1 + lane) & (col == 0) & cross_plane
    to_spare = (last_row - 1 - lane) * RUN
    from_spare = n_chip - (1 + lane) * RUN
    own_skip = (col == RUN - 1) & (own_row | edge_near)
    relay_up = (col == 1) | chained | edge_near
    relay_two = direct
    relay_three = (top & (col == 1)) | chained_two | direct
    far_three = edge_far & jnp.logical_not(plane_out)
    relay_down = inner & (col == 1)

    barrier = pltpu.get_barrier_semaphore()

    def greet(cond, target):
        @pl.when(cond)
        def _():
            pl.semaphore_signal(barrier, inc=1, device_id=core(target), device_id_type=MESH)

    head_of_block = top & (col == 0)
    has_back = ctx > 0
    greet((chip >= 1) & jnp.logical_not(head_of_block & (lane == 0)), -1)
    greet(inner, -RUN)
    greet((inner & (col == 1)) | (top & (col == 1) & has_back & (lane == 1)), -2)
    greet(inner & (col == 0), 1)
    greet(keeper, to_keeper)
    greet(spare_keeper, to_spare)
    greet(head_of_block & has_back & plane_in, -from_spare)
    greet(head_of_block & has_back & (lane == 0), -from_keeper)
    pl.semaphore_signal(barrier, inc=1, device_id=pair_id, device_id_type=MESH)
    expected = (
        1
        + own_next.astype(jnp.int32)
        + own_row.astype(jnp.int32)
        + own_skip.astype(jnp.int32)
        + relay_down.astype(jnp.int32)
        + edge_far.astype(jnp.int32)
        + keeper.astype(jnp.int32)
        + spare_source.astype(jnp.int32)
        + spare_keeper.astype(jnp.int32)
    )
    pl.semaphore_wait(barrier, expected)

    def send_own(h):
        own_load(h, 0).wait()
        own_load(h, 1).wait()

        @pl.when(own_next)
        def _():
            push(h, 6, 4, 0, 1).start()

        @pl.when(spare_source)
        def _():
            push_spare(h).start()

        @pl.when(edge_far)
        def _():
            push_held(h, 6, 0).start()

        @pl.when(own_skip)
        def _():
            push(h, 6, 2, 2, 2).start()

        @pl.when(own_row)
        def _():
            push(h, 6, 0, 1, 3).start()

        @pl.when(lane == 0)
        def _():
            across(h, 0).start()

    def received(h, slot):
        push(h, 6, slot, 0, 0).wait_recv()

    late_edge = edge & cross_plane
    early_own = (row == last_row) & (col == 1) & cross_plane
    upfront = jnp.where(((col == 1) & inner & jnp.logical_not(early_own)) | edge, AHEAD, KV)

    def first_sends(h, carry):
        send_own(h)
        return carry

    lax.fori_loop(0, upfront, first_sends, 0)

    doc_load.wait()
    own_doc = docs[pl.ds(chunk, 1), :]
    query_doc = jnp.transpose(jnp.broadcast_to(own_doc, (CHUNK, CHUNK)))
    i = lax.broadcasted_iota(jnp.int32, (CHUNK, CHUNK), 0)
    j = lax.broadcasted_iota(jnp.int32, (CHUNK, CHUNK), 1)
    for slot in range(SLOTS):
        where = chunk - (BACK - slot)
        key_doc = docs[pl.ds(jnp.maximum(where, 0), 1), :]
        visible = query_doc == jnp.broadcast_to(key_doc, (CHUNK, CHUNK))
        if slot == BACK:
            visible = visible & (j <= i)
        else:
            visible = visible & (jnp.broadcast_to(where, (CHUNK, CHUNK)) >= 0)
        bias[:, slot * CHUNK : (slot + 1) * CHUNK] = jnp.where(visible, 0.0, -1e30).astype(jnp.float32)
    q_load.wait()

    def out_copy(h):
        cols = pl.ds(pl.multiple_of(h * (PER * HEAD), PER * HEAD), PER * HEAD)
        return pltpu.make_async_copy(obuf.at[:, cols], o_hbm.at[:, cols], out_sem.at[h])

    def attend(h):
        base = h * (PER * HEAD)
        q_all = jnp.concatenate(
            [qbuf[:, pl.ds(pl.multiple_of(base + r * HEAD, HEAD), HEAD)] for r in range(PER)], axis=0
        )
        for part in range(0, PER * CHUNK, 384):
            for first in range(0, WINDOW, 256):
                width = min(256, WINDOW - first)
                block = lax.dot_general(
                    q_all[part : part + 384], kv[h, 0, first : first + width, :], (((1,), (1,)), ((), ())),
                    preferred_element_type=jnp.float32,
                )
                for r in range(0, 384, CHUNK):
                    s_ref[part + r : part + r + CHUNK, first : first + width] = (
                        block[r : r + CHUNK] * SCALE2 + bias[:, first : first + width]
                    )
        done = []
        for top_row in range(0, PER * CHUNK, 384):
            totals = []
            for r in range(top_row, top_row + 384, 32):
                scores = s_ref[r : r + 32, :]
                weights = jnp.exp2(scores - jnp.max(scores, axis=-1, keepdims=True))
                totals.append(jnp.sum(weights, axis=-1, keepdims=True))
                p_ref[r : r + 32, :] = weights.astype(jnp.bfloat16)
            mixed = jnp.dot(p_ref[top_row : top_row + 384, :], kv[h, 1], preferred_element_type=jnp.float32)
            done.append((mixed / jnp.concatenate(totals, axis=0)).astype(jnp.bfloat16))
        done = jnp.concatenate(done, axis=0)
        for r in range(PER):
            obuf[:, pl.ds(pl.multiple_of(base + r * HEAD, HEAD), HEAD)] = done[r * CHUNK : (r + 1) * CHUNK]
        out_copy(h).start()

    def on_near(h):
        @pl.when(chip >= 1)
        def _():
            received(h, 4)

            @pl.when(relay_up)
            def _():
                push(h, 4, 2, 3, 1).start()

            @pl.when(edge_far)
            def _():
                push_held(h, 4, 3).start()

            @pl.when(relay_two)
            def _():
                push(h, 4, 0, 4, 2).start()

            across(h, 1 - lane).start()

    def on_middle(h):
        @pl.when(chip >= 2)
        def _():
            received(h, 2)

            @pl.when(relay_three)
            def _():
                push(h, 2, 0, 5, 1).start()

            @pl.when(far_three)
            def _():
                push_held(h, 2, 5).start()

            across(h, 2 - lane).start()

    def on_far(h):
        @pl.when(chip >= 3)
        def _():
            received(h, 0)

            @pl.when(relay_down)
            def _():
                push(h, 0, 2, 6, -1).start()

            @pl.when(lane == 1)
            def _():
                across(h, 2).start()

    def on_held(h, index):
        push_held(h, 2 * index + 2, 0).wait_recv()
        release(h, index).start()

    def on_spare(h):
        push_spare(h).wait_recv()
        release_spare(h).start()

    def inside(h):
        return (h >= 0) & (h < KV)

    def at(t, lag, action, extra=None):
        h = t - lag
        cond = inside(h) if extra is None else inside(h) & extra

        @pl.when(cond)
        def _():
            action(h)

    lag_near = jnp.where(top, LAGS_TOP[0], LAGS_IN[0])
    lag_middle = jnp.where(top, LAGS_TOP[1], jnp.where(late_edge, LAG_LATE, LAGS_IN[1]))
    lag_far = jnp.where(top, LAGS_TOP[2], jnp.where(late_edge, LAG_LATE, LAGS_IN[2]))
    lag_attend = jnp.where(top, LAGS_TOP[3], jnp.where(late_edge, LAG_LATE + 1, LAGS_IN[3]))

    def finish(h):
        for stage in range(3):
            @pl.when(chip >= stage + 1 - lane)
            def _():
                across(h, stage).wait_recv()
        attend(h)

    def step(t, carry):
        at(t, -upfront, send_own)
        at(t, lag_near, on_near)
        at(2 * t, 0, on_spare, spare_keeper)
        at(2 * t, -1, on_spare, spare_keeper)
        at(t, LAGS_HELD[2], lambda h: on_held(h, 2), keeper & jnp.logical_not(plane_out))
        at(t, LAGS_HELD[1], lambda h: on_held(h, 1), keeper & jnp.logical_not(plane_out))
        for more in range(2):
            at(2 * t, -more, lambda h: on_held(h, 2), keeper & plane_out)
            at(2 * t, 1 - more, lambda h: on_held(h, 1), keeper & plane_out)
        at(t, LAGS_HELD[0], lambda h: on_held(h, 0), keeper & jnp.logical_not(plane_out))
        at(t, lag_far, on_far, inner)
        at(t, lag_middle, on_middle)
        at(t, lag_far, on_far, top)
        at(t, lag_attend, finish)
        return carry

    lax.fori_loop(0, KV + jnp.maximum(lag_attend, LAGS_HELD[0]), step, 0)

    def drain(h, carry):
        sends = (
            (0, own_next | edge_far), (1, own_row), (2, own_skip | spare_source),
            (3, (chip >= 1) & (relay_up | edge_far)), (4, relay_two),
            (5, (chip >= 2) & (relay_three | far_three)), (6, relay_down),
        )
        for index, cond in sends:
            @pl.when(cond)
            def _():
                push(h, 6, 4, index, 0).wait_send()

        for index in range(3):
            held_here = keeper if index else (keeper & jnp.logical_not(plane_out)) | spare_keeper

            @pl.when(held_here)
            def _():
                release(h, index).wait_send()

        for stage in range(3):
            @pl.when(chip >= stage + lane)
            def _():
                across(h, stage).wait_send()

        out_copy(h).wait()
        return carry

    lax.fori_loop(0, KV, drain, 0)


def shards(n_ctx, n_chip, queries, keys, values, doc_ids):
    tokens = queries.shape[0]
    anywhere = pl.BlockSpec(memory_space=pl.ANY)
    docs = doc_ids.reshape(-1, CHUNK)
    return pl.pallas_call(
        lambda *refs: kernel(n_ctx, n_chip, *refs),
        out_shape=jax.ShapeDtypeStruct((tokens, HQ * HEAD), jnp.bfloat16),
        in_specs=[anywhere] * 4,
        out_specs=anywhere,
        scratch_shapes=[
            pltpu.VMEM((KV, 2, WINDOW, HEAD), jnp.bfloat16),
            pltpu.VMEM((KV, 3, 2, CHUNK, HEAD), jnp.bfloat16),
            pltpu.VMEM((CHUNK, HQ * HEAD), jnp.bfloat16),
            pltpu.VMEM((CHUNK, HQ * HEAD), jnp.bfloat16),
            pltpu.VMEM(docs.shape, jnp.int32),
            pltpu.VMEM((CHUNK, WINDOW), jnp.float32),
            pltpu.VMEM((PER * CHUNK, WINDOW), jnp.float32),
            pltpu.VMEM((PER * CHUNK, WINDOW), jnp.bfloat16),
            pltpu.SemaphoreType.DMA((2, KV)),
            pltpu.SemaphoreType.DMA,
            pltpu.SemaphoreType.DMA,
            pltpu.SemaphoreType.DMA((7, KV)),
            pltpu.SemaphoreType.DMA((3, KV)),
            pltpu.SemaphoreType.DMA((3, KV)),
            pltpu.SemaphoreType.DMA((BACK, KV)),
            pltpu.SemaphoreType.DMA((3, KV)),
            pltpu.SemaphoreType.DMA((KV,)),
        ],
        compiler_params=pltpu.CompilerParams(
            collective_id=0, has_side_effects=True, vmem_limit_bytes=56 * 1024 * 1024
        ),
        name="halo_attention",
    )(queries, keys, values, docs)


def solution(mesh):
    placed = (
        P(("ctx", "ulysses"), None),
        P(("ctx", "ulysses"), None),
        P(("ctx", "ulysses"), None),
        P(),
    )
    n_ctx, n_chip = mesh.shape["ctx"], mesh.shape["ulysses"] // 2
    return jax.shard_map(
        lambda *arrays: shards(n_ctx, n_chip, *arrays),
        mesh=mesh, in_specs=placed, out_specs=P(("ctx", "ulysses"), None), check_vma=False,
    )
```

```python
import math

import jax
import jax.numpy as jnp
from jax import lax
from jax.experimental import pallas as pl
from jax.experimental.pallas import tpu as pltpu
from jax.sharding import PartitionSpec as P

HQ = 48
KV = 8
HEAD = 128
PER = HQ // KV
CHUNK = 128
BACK = 6
SLOTS = BACK + 1
WINDOW = SLOTS * CHUNK
SCALE2 = math.log2(math.e) / math.sqrt(HEAD)
RUN = 3
LAGS_IN = (0, 2, 1, 3)
LAGS_TOP = (1, 3, 5, 6)
AHEAD = 3
LAGS_HELD = (3, 1, 0)
LAG_LATE = 8
TURNS = 4
MESH = pl.DeviceIdType.MESH


def kernel(
    n_ctx, n_chip, q_hbm, k_hbm, v_hbm, doc_hbm, o_hbm,
    kv, held, qbuf, obuf, docs, bias, s_ref, p_ref,
    load_sem, q_sem, doc_sem, push_send, held_send, pair_send, recv_sem, held_recv, out_sem,
):
    ctx = lax.axis_index("ctx")
    uly = lax.axis_index("ulysses")
    lane = lax.rem(uly, 2)
    place = uly // 2
    row, col = place // RUN, lax.rem(place, RUN)
    last_row = n_chip // RUN - 1
    chip = ctx * n_chip + place
    chunk = chip * 2 + lane
    top, inner = row == 0, row > 0
    edge = (row == last_row) & (col == RUN - 1)
    onward = ctx < n_ctx - 1
    edge_far = edge & onward & (lane == 0)
    edge_near = edge & onward & (lane == 1)
    keeper = (row == 1) & (col == RUN - 1) & onward & (lane == 0)
    to_keeper = n_chip - 2 * RUN
    from_keeper = n_chip - 2 * RUN + 1

    def core(away):
        there = place + away
        wrap = (there >= n_chip).astype(jnp.int32) - (there < 0).astype(jnp.int32)
        return (ctx + wrap, uly + 2 * away - 2 * n_chip * wrap)

    pair_id = (ctx, uly + 1 - 2 * lane)

    def own_load(h, part):
        src = (k_hbm, v_hbm)[part]
        return pltpu.make_async_copy(
            src.at[:, pl.ds(pl.multiple_of(h * HEAD, HEAD), HEAD)],
            kv.at[h, part, pl.ds(BACK * CHUNK, CHUNK), :],
            load_sem.at[part, h],
        )

    def start_loads(h, carry):
        own_load(h, 0).start()
        own_load(h, 1).start()
        return carry

    lax.fori_loop(0, KV, start_loads, 0)
    doc_load = pltpu.make_async_copy(doc_hbm, docs, doc_sem)
    doc_load.start()
    q_load = pltpu.make_async_copy(q_hbm, qbuf, q_sem)
    q_load.start()

    @pl.when(chip < 3)
    def _():
        def clear(h, carry):
            for part in range(2):
                kv[h, part, : BACK * CHUNK, :] = jnp.zeros((BACK * CHUNK, HEAD), jnp.bfloat16)
            return carry

        lax.fori_loop(0, KV, clear, 0)

    def rows(slot):
        return pl.ds(pl.multiple_of(slot * CHUNK, CHUNK), CHUNK)

    def push(h, src, dst, index, target):
        return pltpu.make_async_remote_copy(
            src_ref=kv.at[h, :, rows(src), :],
            dst_ref=kv.at[h, :, rows(dst), :],
            send_sem=push_send.at[index, h],
            recv_sem=recv_sem.at[dst, h],
            device_id=core(target),
            device_id_type=MESH,
        )

    def push_spare(h):
        return pltpu.make_async_remote_copy(
            src_ref=kv.at[h, :, rows(6), :],
            dst_ref=held.at[h, 0],
            send_sem=push_send.at[2, h],
            recv_sem=held_recv.at[0, h],
            device_id=core(-to_spare),
            device_id_type=MESH,
        )

    def release_spare(h):
        return pltpu.make_async_remote_copy(
            src_ref=held.at[h, 0],
            dst_ref=kv.at[h, :, rows(0), :],
            send_sem=held_send.at[0, h],
            recv_sem=recv_sem.at[0, h],
            device_id=core(from_spare),
            device_id_type=MESH,
        )

    def push_held(h, src, index):
        return pltpu.make_async_remote_copy(
            src_ref=kv.at[h, :, rows(src), :],
            dst_ref=held.at[h, src // 2 - 1],
            send_sem=push_send.at[index, h],
            recv_sem=held_recv.at[src // 2 - 1, h],
            device_id=core(-to_keeper),
            device_id_type=MESH,
        )

    def release(h, index):
        dst = 2 * index
        return pltpu.make_async_remote_copy(
            src_ref=held.at[h, index],
            dst_ref=kv.at[h, :, rows(dst), :],
            send_sem=held_send.at[index, h],
            recv_sem=recv_sem.at[dst, h],
            device_id=core(from_keeper),
            device_id_type=MESH,
        )

    def across(h, stage):
        src, dst = BACK - 2 * stage - 2 * lane, BACK - 2 * stage - 1
        return pltpu.make_async_remote_copy(
            src_ref=kv.at[h, :, rows(src), :],
            dst_ref=kv.at[h, :, rows(dst), :],
            send_sem=pair_send.at[stage, h],
            recv_sem=recv_sem.at[dst, h],
            device_id=pair_id,
            device_id_type=MESH,
        )

    own_next = jnp.logical_not(edge) | edge_near
    own_row = row < last_row
    plane_out = lax.rem(ctx, TURNS) == TURNS - 1
    plane_in = lax.rem(ctx, TURNS) == 0
    direct = edge_near & jnp.logical_not(plane_out)
    chained = top & (col == 0) & (lane == 0)
    chained_two = top & (col == 0) & ((lane == 0) | plane_in)
    cross_plane = plane_out & onward
    spare_source = (row == last_row) & (col == 0) & cross_plane
    spare_keeper = (row == 1 + lane) & (col == 0) & cross_plane
    to_spare = (last_row - 1 - lane) * RUN
    from_spare = n_chip - (1 + lane) * RUN
    own_skip = (col == RUN - 1) & (own_row | edge_near)
    relay_up = (col == 1) | chained | edge_near
    relay_two = direct
    relay_three = (top & (col == 1)) | chained_two | direct
    far_three = edge_far & jnp.logical_not(plane_out)
    relay_down = inner & (col == 1)

    barrier = pltpu.get_barrier_semaphore()

    def greet(cond, target):
        @pl.when(cond)
        def _():
            pl.semaphore_signal(barrier, inc=1, device_id=core(target), device_id_type=MESH)

    head_of_block = top & (col == 0)
    has_back = ctx > 0
    greet((chip >= 1) & jnp.logical_not(head_of_block & (lane == 0)), -1)
    greet(inner, -RUN)
    greet((inner & (col == 1)) | (top & (col == 1) & has_back & (lane == 1)), -2)
    greet(inner & (col == 0), 1)
    greet(keeper, to_keeper)
    greet(spare_keeper, to_spare)
    greet(head_of_block & has_back & plane_in, -from_spare)
    greet(head_of_block & has_back & (lane == 0), -from_keeper)
    pl.semaphore_signal(barrier, inc=1, device_id=pair_id, device_id_type=MESH)
    expected = (
        1
        + own_next.astype(jnp.int32)
        + own_row.astype(jnp.int32)
        + own_skip.astype(jnp.int32)
        + relay_down.astype(jnp.int32)
        + edge_far.astype(jnp.int32)
        + keeper.astype(jnp.int32)
        + spare_source.astype(jnp.int32)
        + spare_keeper.astype(jnp.int32)
    )
    pl.semaphore_wait(barrier, expected)

    def send_own(h):
        own_load(h, 0).wait()
        own_load(h, 1).wait()

        @pl.when(own_next)
        def _():
            push(h, 6, 4, 0, 1).start()

        @pl.when(spare_source)
        def _():
            push_spare(h).start()

        @pl.when(edge_far)
        def _():
            push_held(h, 6, 0).start()

        @pl.when(own_skip)
        def _():
            push(h, 6, 2, 2, 2).start()

        @pl.when(own_row)
        def _():
            push(h, 6, 0, 1, 3).start()

        @pl.when(lane == 0)
        def _():
            across(h, 0).start()

    def received(h, slot):
        push(h, 6, slot, 0, 0).wait_recv()

    late_edge = edge & cross_plane
    early_own = (row == last_row) & (col == 1) & cross_plane
    upfront = jnp.where(((col == 1) & inner & jnp.logical_not(early_own)) | edge | spare_keeper, AHEAD, KV)

    def first_sends(h, carry):
        send_own(h)
        return carry

    lax.fori_loop(0, upfront, first_sends, 0)

    doc_load.wait()
    own_doc = docs[pl.ds(chunk, 1), :]
    query_doc = jnp.transpose(jnp.broadcast_to(own_doc, (CHUNK, CHUNK)))
    i = lax.broadcasted_iota(jnp.int32, (CHUNK, CHUNK), 0)
    j = lax.broadcasted_iota(jnp.int32, (CHUNK, CHUNK), 1)
    for slot in range(SLOTS):
        where = chunk - (BACK - slot)
        key_doc = docs[pl.ds(jnp.maximum(where, 0), 1), :]
        visible = query_doc == jnp.broadcast_to(key_doc, (CHUNK, CHUNK))
        if slot == BACK:
            visible = visible & (j <= i)
        else:
            visible = visible & (jnp.broadcast_to(where, (CHUNK, CHUNK)) >= 0)
        bias[:, slot * CHUNK : (slot + 1) * CHUNK] = jnp.where(visible, 0.0, -1e30).astype(jnp.float32)
    q_load.wait()

    def out_copy(h):
        cols = pl.ds(pl.multiple_of(h * (PER * HEAD), PER * HEAD), PER * HEAD)
        return pltpu.make_async_copy(obuf.at[:, cols], o_hbm.at[:, cols], out_sem.at[h])

    def attend(h):
        base = h * (PER * HEAD)
        q_all = jnp.concatenate(
            [qbuf[:, pl.ds(pl.multiple_of(base + r * HEAD, HEAD), HEAD)] for r in range(PER)], axis=0
        )
        for part in range(0, PER * CHUNK, 384):
            for first in range(0, WINDOW, 256):
                width = min(256, WINDOW - first)
                block = lax.dot_general(
                    q_all[part : part + 384], kv[h, 0, first : first + width, :], (((1,), (1,)), ((), ())),
                    preferred_element_type=jnp.float32,
                )
                for r in range(0, 384, CHUNK):
                    s_ref[part + r : part + r + CHUNK, first : first + width] = (
                        block[r : r + CHUNK] * SCALE2 + bias[:, first : first + width]
                    )
        done = []
        for top_row in range(0, PER * CHUNK, 384):
            totals = []
            for r in range(top_row, top_row + 384, 32):
                scores = s_ref[r : r + 32, :]
                weights = jnp.exp2(scores - jnp.max(scores, axis=-1, keepdims=True))
                totals.append(jnp.sum(weights, axis=-1, keepdims=True))
                p_ref[r : r + 32, :] = weights.astype(jnp.bfloat16)
            mixed = jnp.dot(p_ref[top_row : top_row + 384, :], kv[h, 1], preferred_element_type=jnp.float32)
            done.append((mixed / jnp.concatenate(totals, axis=0)).astype(jnp.bfloat16))
        done = jnp.concatenate(done, axis=0)
        for r in range(PER):
            obuf[:, pl.ds(pl.multiple_of(base + r * HEAD, HEAD), HEAD)] = done[r * CHUNK : (r + 1) * CHUNK]
        out_copy(h).start()

    def on_near(h):
        @pl.when(chip >= 1)
        def _():
            received(h, 4)

            @pl.when(relay_up)
            def _():
                push(h, 4, 2, 3, 1).start()

            @pl.when(edge_far)
            def _():
                push_held(h, 4, 3).start()

            @pl.when(relay_two)
            def _():
                push(h, 4, 0, 4, 2).start()

            across(h, 1 - lane).start()

    def on_middle(h):
        @pl.when(chip >= 2)
        def _():
            received(h, 2)

            @pl.when(relay_three)
            def _():
                push(h, 2, 0, 5, 1).start()

            @pl.when(far_three)
            def _():
                push_held(h, 2, 5).start()

            across(h, 2 - lane).start()

    def on_far(h):
        @pl.when(chip >= 3)
        def _():
            received(h, 0)

            @pl.when(relay_down)
            def _():
                push(h, 0, 2, 6, -1).start()

            @pl.when(lane == 1)
            def _():
                across(h, 2).start()

    def on_held(h, index):
        push_held(h, 2 * index + 2, 0).wait_recv()
        release(h, index).start()

    def on_spare(h):
        push_spare(h).wait_recv()
        release_spare(h).start()

    def inside(h):
        return (h >= 0) & (h < KV)

    def at(t, lag, action, extra=None):
        h = t - lag
        cond = inside(h) if extra is None else inside(h) & extra

        @pl.when(cond)
        def _():
            action(h)

    lag_near = jnp.where(top, LAGS_TOP[0], LAGS_IN[0])
    lag_middle = jnp.where(top, LAGS_TOP[1], jnp.where(late_edge, LAG_LATE, LAGS_IN[1]))
    lag_far = jnp.where(top, LAGS_TOP[2], jnp.where(late_edge, LAG_LATE, LAGS_IN[2]))
    lag_attend = jnp.where(top, LAGS_TOP[3], jnp.where(late_edge, LAG_LATE + 1, LAGS_IN[3]))

    def finish(h):
        for stage in range(3):
            @pl.when(chip >= stage + 1 - lane)
            def _():
                across(h, stage).wait_recv()
        attend(h)

    def step(t, carry):
        at(t, -upfront, send_own)
        at(t, lag_near, on_near)
        at(2 * t, 0, on_spare, spare_keeper)
        at(2 * t, -1, on_spare, spare_keeper)
        at(t, LAGS_HELD[2], lambda h: on_held(h, 2), keeper & jnp.logical_not(plane_out))
        at(t, LAGS_HELD[1], lambda h: on_held(h, 1), keeper & jnp.logical_not(plane_out))
        for more in range(2):
            at(2 * t, -more, lambda h: on_held(h, 2), keeper & plane_out)
            at(2 * t, 1 - more, lambda h: on_held(h, 1), keeper & plane_out)
        at(t, LAGS_HELD[0], lambda h: on_held(h, 0), keeper & jnp.logical_not(plane_out))
        at(t, lag_far, on_far, inner)
        at(t, lag_middle, on_middle)
        at(t, lag_far, on_far, top)
        at(t, lag_attend, finish)
        return carry

    lax.fori_loop(0, KV + jnp.maximum(lag_attend, LAGS_HELD[0]), step, 0)

    def drain(h, carry):
        sends = (
            (0, own_next | edge_far), (1, own_row), (2, own_skip | spare_source),
            (3, (chip >= 1) & (relay_up | edge_far)), (4, relay_two),
            (5, (chip >= 2) & (relay_three | far_three)), (6, relay_down),
        )
        for index, cond in sends:
            @pl.when(cond)
            def _():
                push(h, 6, 4, index, 0).wait_send()

        for index in range(3):
            held_here = keeper if index else (keeper & jnp.logical_not(plane_out)) | spare_keeper

            @pl.when(held_here)
            def _():
                release(h, index).wait_send()

        for stage in range(3):
            @pl.when(chip >= stage + lane)
            def _():
                across(h, stage).wait_send()

        out_copy(h).wait()
        return carry

    lax.fori_loop(0, KV, drain, 0)


def shards(n_ctx, n_chip, queries, keys, values, doc_ids):
    tokens = queries.shape[0]
    anywhere = pl.BlockSpec(memory_space=pl.ANY)
    docs = doc_ids.reshape(-1, CHUNK)
    return pl.pallas_call(
        lambda *refs: kernel(n_ctx, n_chip, *refs),
        out_shape=jax.ShapeDtypeStruct((tokens, HQ * HEAD), jnp.bfloat16),
        in_specs=[anywhere] * 4,
        out_specs=anywhere,
        scratch_shapes=[
            pltpu.VMEM((KV, 2, WINDOW, HEAD), jnp.bfloat16),
            pltpu.VMEM((KV, 3, 2, CHUNK, HEAD), jnp.bfloat16),
            pltpu.VMEM((CHUNK, HQ * HEAD), jnp.bfloat16),
            pltpu.VMEM((CHUNK, HQ * HEAD), jnp.bfloat16),
            pltpu.VMEM(docs.shape, jnp.int32),
            pltpu.VMEM((CHUNK, WINDOW), jnp.float32),
            pltpu.VMEM((PER * CHUNK, WINDOW), jnp.float32),
            pltpu.VMEM((PER * CHUNK, WINDOW), jnp.bfloat16),
            pltpu.SemaphoreType.DMA((2, KV)),
            pltpu.SemaphoreType.DMA,
            pltpu.SemaphoreType.DMA,
            pltpu.SemaphoreType.DMA((7, KV)),
            pltpu.SemaphoreType.DMA((3, KV)),
            pltpu.SemaphoreType.DMA((3, KV)),
            pltpu.SemaphoreType.DMA((BACK, KV)),
            pltpu.SemaphoreType.DMA((3, KV)),
            pltpu.SemaphoreType.DMA((KV,)),
        ],
        compiler_params=pltpu.CompilerParams(
            collective_id=0, has_side_effects=True, vmem_limit_bytes=56 * 1024 * 1024
        ),
        name="halo_attention",
    )(queries, keys, values, docs)


def solution(mesh):
    placed = (
        P(("ctx", "ulysses"), None),
        P(("ctx", "ulysses"), None),
        P(("ctx", "ulysses"), None),
        P(),
    )
    n_ctx, n_chip = mesh.shape["ctx"], mesh.shape["ulysses"] // 2
    return jax.shard_map(
        lambda *arrays: shards(n_ctx, n_chip, *arrays),
        mesh=mesh, in_specs=placed, out_specs=P(("ctx", "ulysses"), None), check_vma=False,
    )
```
